32 devices in a mesh: dp: 2 (over x), expert: 16 (over z, y, core).
Axes of the slice: x: 2, y: 2, z: 4, core: 2. Of those that a mesh axis runs over, the one named last changes fastest.
Arguments:
- tokens: bfloat16 [2048, 2048], P(('dp', 'expert')), may hold values from -6 to 6
- cotangent: bfloat16 [2048, 2048], P(('dp', 'expert')), may hold values from -6 to 6
- expert_ids: int32 [2048, 8], P(('dp', 'expert')), may hold values from 0 to 15, all different within a row
- gate_probs: float32 [2048, 8], P(('dp', 'expert')), may hold values from 0.05 to 0.5
- held_before: int32 [16], replicated, may hold values from 0 to 15, each once
- swap_flags: int32 [8], replicated, may hold values from 0 to 1, as said below
- weights: bfloat16 [16, 2048, 3, 384], P('expert'), may hold values from -0.125 to 0.125
Outputs:
- mixed: bfloat16 [2048, 2048], P(('dp', 'expert'))
- token_grads: bfloat16 [2048, 2048], P(('dp', 'expert'))
- gate_grads: float32 [2048, 8], P(('dp', 'expert'))
- weight_grads: float32 [16, 2048, 3, 384], P('expert', 'dp')
The draws below stay inside these ranges and needn't reach their ends.
Inputs may be any that keep to these rules, and one draw needn't show every extreme that they name: `expert_ids`: each row names 8 different experts. `held_before`: each expert once. `swap_flags`: entry 0 is always 1; the others are 0 or 1.
All inputs are finite; a program needn't handle non-finite values.
Results may differ from the reference program's by a relative error of at most 0.013.
Values may be sent and summed in bfloat16 or wider, within the bound.
No kernel may reach another device: no remote copies, remote signals or barrier semaphores. Data moves between devices by JAX's collectives and lax.ppermute only.
A program may use at most 64 MiB of HBM per device.

```python
import jax
import jax.numpy as jnp
from jax import lax

D = 2048
FF = 384
TOP = 8
TOK_DEV = 64
EXPERTS = 16
CAP = 32
REPLICAS = 2
TOKENS = 2048


def draw_swap_flags(key, part):
    flags = jax.random.randint(jax.random.fold_in(key, 71), (EXPERTS // 2,), 0, 2).astype(jnp.int32)
    return flags.at[0].set(1)


def levels(stream_key, shape, cuts, least, largest):
    loudness = 1.0
    for axis_at, shards_of in cuts:
        draws = jax.random.uniform(jax.random.fold_in(jax.random.fold_in(stream_key, 6), axis_at), (shards_of,), jnp.float32, least / len(cuts), largest / len(cuts))
        loudness = loudness * jnp.repeat(jnp.exp(draws), shape[axis_at] // shards_of).reshape((-1,) + (1,) * (len(shape) - 1 - axis_at))
    return loudness


def picks_of(own_key, rows, number_of, top, lift):
    order = jax.random.permutation(jax.random.fold_in(own_key, 1), number_of)
    pull = order
    for power in range(3):
        pull = pull * pull // number_of
    pull = pull * lift // number_of
    chance = jax.random.randint(jax.random.fold_in(own_key, 2), (rows, number_of), 0, 4096) + pull
    fixed_rows = jax.random.permutation(jax.random.fold_in(own_key, 3), rows)[jnp.arange(number_of) % rows]
    chance = jnp.where(jnp.arange(rows)[:, None] == fixed_rows[None, :], 1 << 14, chance)
    merit = chance * number_of + jnp.arange(number_of)
    return lax.top_k(merit.astype(jnp.int32), top)[1].astype(jnp.int32)


def centred(rng, extent, spread, bound, pieces=(), held_as=jnp.bfloat16):
    values = jax.random.normal(rng, extent, jnp.float32) * spread
    if len(pieces) > 0:
        values = levels(rng, extent, pieces, -0.22, 0.18) * values
    return jnp.clip(values, min=-bound, max=bound).astype(held_as)


def setup_inputs(seed: int = 0) -> dict:
    keys = jax.random.split(jax.random.key(seed), 8)
    return {
        "tokens": centred(keys[0], (TOKENS, D), 1.0, 6.0, ((0, 32),)),
        "cotangent": centred(keys[1], (TOKENS, D), 1.0, 6.0, ((0, 32),)),
        "expert_ids": picks_of(keys[2], TOKENS, EXPERTS, TOP, 8192),
        "gate_probs": jnp.clip(0.05 + 0.45 * jax.random.uniform(keys[3], (TOKENS, TOP), jnp.float32) ** levels(keys[3], (TOKENS, TOP), ((0, 32),), -0.2, 0.2), 0.05, 0.5),
        "held_before": jax.random.permutation(keys[4], EXPERTS).astype(jnp.int32),
        "swap_flags": draw_swap_flags(jax.random.fold_in(keys[7], 71), 0),
        "weights": centred(keys[6], (EXPERTS, D, 3, FF), D ** -0.5, 0.125, ((0, 16),)),
    }


def silu_terms(gate):
    sigma = jax.nn.sigmoid(gate)
    return gate * sigma, sigma * (1.0 + gate * (1.0 - sigma))


def replica_sum(left, right):
    product = jnp.einsum("prd,prf->pdf", left.reshape(REPLICAS, -1, D).astype(jnp.float32), right.reshape(REPLICAS, -1, FF).astype(jnp.float32))
    product = lax.optimization_barrier(product.astype(jnp.bfloat16))
    return jnp.sum(product.astype(jnp.float32), axis=0)


def reference(tokens, cotangent, expert_ids, gate_probs, held_before, swap_flags, weights):
    total_rows = (TOKENS // TOK_DEV) * CAP
    labels = jnp.arange(EXPERTS, dtype=jnp.int32)
    onehot = (expert_ids[:, :, None] == labels[None, None, :]).astype(jnp.int32)
    per_token = jnp.sum(onehot, axis=1).reshape(-1, TOK_DEV, EXPERTS)
    earlier = (jnp.cumsum(per_token, axis=1) - per_token).reshape(TOKENS, EXPERTS)
    rank = jnp.sum(onehot * earlier[:, None, :], axis=2)
    group = jnp.arange(TOKENS, dtype=jnp.int32) // TOK_DEV
    slot_of = jnp.sum((held_before[None, :] == labels[:, None]).astype(jnp.int32) * labels[None, :], axis=1)
    flags_all = jnp.concatenate([swap_flags, swap_flags])
    held_after = jnp.where(flags_all == 1, jnp.roll(held_before, EXPERTS // 2), held_before)
    cot_wide = cotangent.astype(jnp.float32)

    def per_expert(carry, expert):
        mixed_sum, grad_sum, gate_sum = carry
        named = (expert_ids == expert) & (rank < CAP)
        present = jnp.any(named, axis=1)
        rank_here = jnp.sum(jnp.where(named, rank, 0), axis=1).astype(jnp.int32)
        prob_here = jnp.sum(jnp.where(named, gate_probs, jnp.float32(0.0)), axis=1)
        row_index = jnp.where(present, group * CAP + rank_here, total_rows).astype(jnp.int32)
        inputs = jnp.zeros((total_rows, D), jnp.bfloat16).at[row_index].set(tokens, mode="drop")
        matrices = lax.dynamic_index_in_dim(weights, slot_of[expert], 0, keepdims=False)
        w_in = matrices[:, :2, :].reshape(D, 2 * FF)
        w_out = matrices[:, 2, :]
        gate_up = jnp.dot(inputs, w_in, preferred_element_type=jnp.float32)
        gate = gate_up[:, :FF]
        up_part = gate_up[:, FF:]
        silu_value, slope = silu_terms(gate)
        hidden = (silu_value * up_part).astype(jnp.bfloat16)
        outputs = lax.dot_general(hidden, w_out, (((1,), (1,)), ((), ())), preferred_element_type=jnp.float32).astype(jnp.bfloat16)
        picked = outputs.at[row_index].get(mode="fill", fill_value=0).astype(jnp.float32)
        mixed_sum = mixed_sum + prob_here[:, None] * picked
        inner = jnp.sum(cot_wide * picked, axis=1)
        gate_sum = gate_sum + jnp.where(named, inner[:, None], jnp.float32(0.0))
        weighted = (prob_here[:, None] * cot_wide).astype(jnp.bfloat16)
        upstream = jnp.zeros((total_rows, D), jnp.bfloat16).at[row_index].set(weighted, mode="drop")
        d_hidden = jnp.dot(upstream, w_out, preferred_element_type=jnp.float32)
        d_gate = (d_hidden * up_part * slope).astype(jnp.bfloat16)
        d_up = (d_hidden * silu_value).astype(jnp.bfloat16)
        back = lax.dot_general(jnp.concatenate([d_gate, d_up], axis=1), w_in, (((1,), (1,)), ((), ())), preferred_element_type=jnp.float32).astype(jnp.bfloat16)
        grad_sum = grad_sum + back.at[row_index].get(mode="fill", fill_value=0).astype(jnp.float32)
        grads = jnp.stack([replica_sum(inputs, d_gate), replica_sum(inputs, d_up), replica_sum(upstream, hidden)], axis=1)
        return (mixed_sum, grad_sum, gate_sum), grads

    start = (jnp.zeros((TOKENS, D), jnp.float32), jnp.zeros((TOKENS, D), jnp.float32), jnp.zeros((TOKENS, TOP), jnp.float32))
    (mixed_sum, grad_sum, gate_sum), grads = lax.scan(per_expert, start, labels)
    weight_grads = jnp.take(grads, held_after, axis=0)
    return mixed_sum.astype(jnp.bfloat16), grad_sum.astype(jnp.bfloat16), gate_sum, weight_grads
```

```python
import functools

import jax
import jax.numpy as jnp
from jax import lax
from jax.experimental import pallas as pl
from jax.experimental.pallas import tpu as pltpu
from jax.sharding import PartitionSpec as P


F32, BF16 = jnp.float32, jnp.bfloat16
TN = (((0,), (0,)), ((), ()))
NN = (((1,), (0,)), ((), ()))
NT = (((1,), (1,)), ((), ()))


def dot(a, b, dims):
    return lax.dot_general(a, b, dims, preferred_element_type=F32)


def local(body, outs, scalars, arrays):
    smem = pl.BlockSpec(memory_space=pltpu.SMEM)
    vmem = pl.BlockSpec(memory_space=pltpu.VMEM)
    return pl.pallas_call(
        body,
        out_shape=[jax.ShapeDtypeStruct(s, d) for s, d in outs],
        in_specs=[smem] * len(scalars) + [vmem] * len(arrays),
        out_specs=[vmem] * len(outs),
    )(*scalars, *arrays)


def split3(value):
    first = value.astype(BF16).astype(F32)
    second = (value - first).astype(BF16).astype(F32)
    return first, second, value - first - second


def lane_of(shape):
    return lax.broadcasted_iota(jnp.int32, shape, 1)


def pick(table, lanes, wanted):
    return jnp.sum(jnp.where(lanes == wanted, table.astype(F32), 0.0), axis=1, keepdims=True)


def prepare(n, capacity, ids, probs, x, out):
    count, top = ids.shape
    width = x.shape[1]
    out[:, :width] = x[...]
    extra = out.shape[1] - width
    lanes = lane_of((count, extra))
    label, field = lanes % n, lanes // n
    named = jnp.zeros((count, extra), F32)
    weight = jnp.zeros((count, extra), F32)
    for k in range(top):
        here = ids[:, k : k + 1] == label
        named = named + jnp.where(here, 1.0, 0.0)
        weight = weight + jnp.where(here, probs[:, k : k + 1], 0.0)
    rows = lax.broadcasted_iota(jnp.int32, (count, count), 0)
    before = jnp.where(lane_of((count, count)) < rows, 1.0, 0.0).astype(BF16)
    rank = dot(before, named.astype(BF16), NN)
    kept = (named > 0.0) & (rank < capacity)
    weight = jnp.where(kept, weight, 0.0)
    first, second, third = split3(weight)
    value = jnp.where(field == 0, jnp.where(kept, rank, -1.0), 0.0)
    for at, part in enumerate((first, second, third)):
        value = jnp.where(field == at + 1, part, value)
    out[:, width:] = value.astype(BF16)


def slots_of(table, n, group, capacity, expert):
    rows = table.shape[0]
    rank = pick(table, lane_of(table.shape), expert)
    at = lax.broadcasted_iota(jnp.int32, (rows, 1), 0) // group
    slot = jnp.where(rank >= 0.0, rank + (at * capacity).astype(F32), -1.0)
    lanes = lane_of((rows, rows // group * capacity)).astype(F32)
    return jnp.where(slot == lanes, 1.0, 0.0).astype(BF16)


def forward(n, group, capacity, held, x_own, x_oth, w, m_own, m_oth, place, hid, slope_w, silu_w, ph):
    expert = held[lax.axis_index("expert")]
    width = w.shape[1]
    for at, (x, m) in enumerate(((x_own, m_own), (x_oth, m_oth))):
        one = slots_of(x[:, width:], n, group, capacity, expert)
        place[at] = one
        packed = dot(one, x[...], TN).astype(BF16)
        table = packed[:, width:]
        lanes = lane_of(table.shape)
        wanted = (lanes == n + expert) | (lanes == 2 * n + expert) | (lanes == 3 * n + expert)
        prob = jnp.sum(jnp.where(wanted, table.astype(F32), 0.0), axis=1, keepdims=True)
        rows = packed[:, :width]
        gate = dot(rows, w[0], NN)
        up = dot(rows, w[1], NN)
        sigma = jax.nn.sigmoid(gate)
        silu = gate * sigma
        hidden = silu * up
        many = one.shape[1]
        span = pl.ds(at * many, many)
        weighted = (prob * hidden).astype(BF16)
        hid[span] = hidden
        slope_w[span] = prob * up * (sigma * (1.0 + gate * (1.0 - sigma)))
        silu_w[span] = prob * silu
        ph[span] = weighted
        outputs = dot(weighted, w[2], NT).astype(BF16)
        m[...] = dot(one, outputs, NN).astype(BF16)


def backward(n, held, c_own, c_oth, w, place, hid, slope_w, silu_w, b_own, b_oth, dg, du):
    expert = held[lax.axis_index("expert")]
    width = w.shape[1]
    for at, (c, b) in enumerate(((c_own, b_own), (c_oth, b_oth))):
        one = place[at]
        many = one.shape[1]
        span = pl.ds(at * many, many)
        rows = dot(one, c[...], TN).astype(BF16)
        d_hidden = dot(rows, w[2], NN)
        d_gate = (d_hidden * slope_w[span]).astype(BF16)
        d_up = (d_hidden * silu_w[span]).astype(BF16)
        dg[span] = d_gate
        du[span] = d_up
        inner = jnp.sum(d_hidden * hid[span], axis=1, keepdims=True)
        back = (dot(d_gate, w[0], NT) + dot(d_up, w[1], NT)).astype(BF16)
        b[:, :width] = dot(one, back, NN).astype(BF16)
        lanes = lane_of((many, b.shape[1] - width))
        value = jnp.zeros(lanes.shape, F32)
        for k, part in enumerate(split3(inner)):
            value = jnp.where(lanes == k * n + expert, part, value)
        b[:, width:] = dot(one, value.astype(BF16), NN).astype(BF16)


def final_expert(held, flags):
    own = lax.axis_index("expert")
    n = held.shape[0]
    moved = flags[own % (n // 2)] == 1
    return moved, jnp.where(moved, held[(own + n // 2) % n], held[own])


def regroup(n, dp, group, capacity, held, flags, *refs):
    xs, cs, (x_out, c_out) = refs[:4], refs[4:8], refs[8:]
    _, expert = final_expert(held, flags)
    share = x_out.shape[2]
    width = share * x_out.shape[0]
    here = lax.axis_index("dp")
    for at, (x, c) in enumerate(zip(xs, cs)):
        one = slots_of(x[:, width:], n, group, capacity, expert)
        many = one.shape[1]
        span = pl.ds(at * many, many)
        for src, dst in ((x, x_out), (c, c_out)):
            for piece in range(x_out.shape[0]):
                start = pl.multiple_of(((here + 1 + piece) % dp) * share, 128)
                dst[piece, span] = dot(one, src[:, pl.ds(start, share)], TN).astype(BF16)


def terms(count, held, flags, rows, *refs):
    moved, _ = final_expert(held, flags)
    near, far, got_near, got_far = (refs[k * count : (k + 1) * count] for k in range(4))
    outs = refs[4 * count :]
    half = rows.shape[1] // 2
    for k in range(count):
        first = jnp.where(moved, got_far[k][...], near[k][...])
        second = jnp.where(moved, got_near[k][...], far[k][...])
        for piece in range(rows.shape[0]):
            out = outs[rows.shape[0] * k + piece]
            value = dot(rows[piece, :half], first, TN) + dot(rows[piece, half:], second, TN)
            out[...] = value.astype(out.dtype)


class Route:
    def __init__(self, n):
        self.low, self.high = n // 4, n // 2
        self.middle = [1 << k for k in range(1, n.bit_length()) if 1 << k < self.low]
        self.every = range(n)
        self.inner = [i for i in self.every if bool(i & self.low) != bool(i & self.high)]
        self.outer = [i for i in self.every if i not in self.inner]

    def swap(self, x, bits, some=None):
        pairs = [(i, i ^ bits) for i in (self.every if some is None else some)]
        return lax.ppermute(x, "expert", pairs)

    def is_inner(self):
        own = lax.axis_index("expert")
        return ((own & self.low) != 0) != ((own & self.high) != 0)

    def gather_near(self, x):
        blocks = [x, self.swap(x, self.low)]
        pair = jnp.concatenate(blocks)
        for bit in self.middle:
            blocks = blocks + [self.swap(b, bit) for b in blocks]
        own = jnp.concatenate(blocks)
        return pair, own, self.swap(own, 1)

    def gather_far(self, pair):
        count = pair.shape[0] // 2
        across = self.swap(pair, self.low | self.high, self.inner)
        onward = self.swap(across, self.low, self.inner)
        turned = jnp.concatenate([across[count:], across[:count]])
        own = jnp.where(self.is_inner(), turned, onward)
        for bit in self.middle:
            own = jnp.concatenate([own, self.swap(own, bit)])
        return own, self.swap(own, 1)

    def fold(self, own, other):
        total = own.astype(F32) + self.swap(other, 1).astype(F32)
        for bit in reversed(self.middle):
            half = total.shape[0] // 2
            got = self.swap(total[half:].astype(BF16), bit)
            total = total[:half] + got.astype(F32)
        return total

    def finish(self, near, far):
        count = near.shape[0] // 2
        got = self.swap(far.astype(BF16), self.low, self.outer).astype(F32)
        first = far[:count] + got[count:]
        second = far[count:] + got[:count]
        leave = jnp.concatenate([second.astype(BF16), first.astype(BF16)])
        near = near + self.swap(leave, self.low | self.high, self.inner).astype(F32)
        return near[:count] + self.swap(near[count:].astype(BF16), self.low).astype(F32)


def on_device(tokens, cotangent, expert_ids, gate_probs, held_before, swap_flags, weights):
    group, width = tokens.shape
    top = expert_ids.shape[1]
    n, dp = lax.axis_size("expert"), lax.axis_size("dp")
    capacity = group * top // n
    ff = weights.shape[3]
    extra = -(-4 * n // 128) * 128
    route = Route(n)
    w = jnp.transpose(weights[0], (1, 0, 2))

    (x,) = local(
        functools.partial(prepare, n, capacity),
        [((group, width + extra), BF16)],
        [],
        [expert_ids, gate_probs, tokens],
    )
    x_pair, *x_near = route.gather_near(x)
    c_pair, *c_near = route.gather_near(cotangent)
    x_far = route.gather_far(x_pair)
    c_far = route.gather_far(c_pair)

    rows = x_near[0].shape[0]
    many = rows // group * capacity

    def run_forward(own, other):
        small = ((2 * many, ff), F32)
        return local(
            functools.partial(forward, n, group, capacity),
            [((rows, width), BF16)] * 2
            + [((2, rows, many), BF16), small, small, small, ((2 * many, ff), BF16)],
            [held_before],
            [own, other, w],
        )

    def run_backward(own, other, state):
        return local(
            functools.partial(backward, n),
            [((rows, width + extra), BF16)] * 2 + [((2 * many, ff), BF16)] * 2,
            [held_before],
            [own, other, w, *state],
        )

    def give(value):
        return route.swap(value, route.high)

    mn_own, mn_oth, *near_state, ph_near = run_forward(*x_near)
    got_ph_near = give(ph_near)
    bn_own, bn_oth, dg_near, du_near = run_backward(*c_near, near_state)
    got_dg_near, got_du_near = give(dg_near), give(du_near)
    mf_own, mf_oth, *far_state, ph_far = run_forward(*x_far)
    got_ph_far = give(ph_far)
    bf_own, bf_oth, dg_far, du_far = run_backward(*c_far, far_state)
    got_dg_far, got_du_far = give(dg_far), give(du_far)

    m_far = route.fold(mf_own, mf_oth)
    m_near = route.fold(mn_own, mn_oth)
    mixed = route.finish(m_near, m_far).astype(BF16)
    b_far = route.fold(bf_own, bf_oth)
    b_near = route.fold(bn_own, bn_oth)
    done = route.finish(b_near, b_far)
    token_grads = done[:, :width].astype(BF16)
    table = sum(done[:, width + k * n : width + (k + 1) * n] for k in range(3))
    labels = jnp.arange(n, dtype=jnp.int32)
    named = expert_ids[:, :, None] == labels[None, None, :]
    gate_grads = jnp.sum(jnp.where(named, table[:, None, :], 0.0), axis=2)

    pieces = 2 if dp == 2 else 1
    share = width // pieces
    x_rows, c_rows = local(
        functools.partial(regroup, n, pieces, group, capacity),
        [((pieces, 4 * many, share), BF16)] * 2,
        [held_before, swap_flags],
        [*x_near, *x_far, *c_near, *c_far],
    )

    def run_terms(data, near, far, got_near, got_far):
        return local(
            functools.partial(terms, len(near)),
            [((share, ff), BF16), ((share, ff), F32)][:pieces] * len(near),
            [held_before, swap_flags],
            [data, *near, *far, *got_near, *got_far],
        )

    down = run_terms(c_rows, [ph_near], [ph_far], [got_ph_near], [got_ph_far])
    both = run_terms(
        x_rows, [dg_near, du_near], [dg_far, du_far], [got_dg_near, got_du_near], [got_dg_far, got_du_far]
    )
    parts = [*both, *down]
    if pieces == 2:
        sums = [
            parts[2 * k + 1] + lax.ppermute(parts[2 * k], "dp", [(0, 1), (1, 0)]).astype(F32)
            for k in range(3)
        ]
        grads = jnp.stack(sums)
    else:
        grads = lax.psum_scatter(jnp.stack(parts), "dp", scatter_dimension=1, tiled=True).astype(F32)
    return mixed, token_grads, gate_grads, jnp.transpose(grads, (1, 0, 2))[None]


def solution(mesh):
    by_token = P(("dp", "expert"), None)
    return jax.shard_map(
        on_device,
        mesh=mesh,
        in_specs=(by_token, by_token, by_token, by_token, P(), P(), P("expert", None, None, None)),
        out_specs=(by_token, by_token, by_token, P("expert", "dp", None, None)),
        check_vma=False,
    )
```
